32 devices in a mesh: pipe: 2 (over x), expert: 16 (over z, y, core).
Axes of the slice: x: 2, y: 2, z: 4, core: 2. Of those that a mesh axis runs over, the one named last changes fastest.
Arguments:
- inputs: bfloat16 [1, 512, 5120], P(None, 'expert'), may hold values from -6 to 6
- router: bfloat16 [2, 5120, 2], P('pipe'), may hold values from -0.078125 to 0.078125
- w_up: bfloat16 [2, 3072, 5120], P('pipe', 'expert'), may hold values from -0.078125 to 0.078125
- w_down: bfloat16 [2, 3072, 5120], P('pipe', 'expert'), may hold values from -0.15625 to 0.15625
- picks: int32 [2, 1, 2, 8], P('pipe'), may hold values from 0 to 511, as said below
- probe: bfloat16 [2, 64, 5120], P('pipe'), may hold values from -0.078125 to 0.078125
Outputs:
- student_feats: bfloat16 [2, 1, 512, 64], P('pipe', None, 'expert')
The draws below stay inside these ranges and needn't reach their ends.
Inputs may be any that keep to these rules, and one draw needn't show every extreme that they name: Each list picks[s, m, e] holds 8 different token positions of the micro-batch. Of the 32 consecutive positions held by one index of expert, at most 1 stand in one list, and in every list some index has exactly 1.
All inputs are finite; a program needn't handle non-finite values.
Results may differ from the reference program's by a relative error of at most 0.0059.
Values may be sent and summed in bfloat16 or wider, within the bound.
A program may use at most 64 MiB of HBM per device.

```python
import jax
import jax.numpy as jnp
from jax import lax

D = 5120
EXPERT_FF = 1536
SPLIT = 8
SLOT = 1
PROJ = 64
TOK_DEV = 32
MICRO = 1
FF_DEV = 192
EXPERTS = 2
SECTIONS = 2
TOKENS = 512
CAP = 8


def draw_picks(key, part):
    sources = TOKENS // TOK_DEV
    tickets = sources * SLOT
    list_count = SECTIONS * MICRO * EXPERTS

    def offset_order(offset_key):
        return jax.random.permutation(offset_key, TOK_DEV)

    def one_list(list_key):
        order_key, first_key, offset_key = jax.random.split(list_key, 3)
        shuffled = jax.random.permutation(order_key, tickets).astype(jnp.int32)
        leading = jax.random.randint(first_key, (), 0, sources).astype(jnp.int32)
        ranks = jnp.arange(tickets, dtype=jnp.int32)
        scores = jnp.where(shuffled // SLOT == leading, ranks - tickets, ranks)
        chosen = shuffled[jnp.argsort(scores)][:CAP]
        offsets = jax.vmap(offset_order)(jax.random.split(offset_key, sources)).astype(jnp.int32)
        owners = chosen // SLOT
        return (owners * TOK_DEV + offsets[owners, chosen % SLOT]).astype(jnp.int32)
    picked = jax.vmap(one_list)(jax.random.split(key, list_count))
    return picked.reshape(SECTIONS, MICRO, EXPERTS, CAP)


def block_scale(key, extent, pieces, smallest, high):
    def one(dim, parts):
        steps = jax.random.uniform(jax.random.fold_in(jax.random.fold_in(key, 6), dim), (parts,), jnp.float32, smallest / len(pieces), high / len(pieces))
        return jnp.repeat(jnp.exp(steps), extent[dim] // parts).reshape((-1,) + (1,) * (len(extent) - dim - 1))

    loudness = one(*pieces[0])
    for cut in pieces[1:]:
        loudness = loudness * one(*cut)
    return loudness


def centred(rng, extent, width, limit, cuts=(), kind=jnp.bfloat16):
    gain = block_scale(rng, extent, cuts, -0.22, 0.18) if cuts else 1.0
    entries = jax.random.normal(rng, extent, jnp.float32) * width * gain
    return jnp.minimum(jnp.maximum(entries, -limit), limit).astype(kind)


def setup_inputs(seed: int = 0) -> dict:
    key_of = jax.random.split(jax.random.key(seed), 7)
    return {
        "inputs": centred(key_of[0], (MICRO, TOKENS, D), 1.0, 6.0, ((1, 16),)),
        "router": centred(key_of[1], (SECTIONS, D, EXPERTS), D ** -0.5, 0.078125, ((0, 2),)),
        "w_up": centred(key_of[2], (SECTIONS, EXPERTS * EXPERT_FF, D), D ** -0.5, 0.078125, ((0, 2), (1, 16))),
        "w_down": centred(key_of[3], (SECTIONS, EXPERTS * EXPERT_FF, D), EXPERT_FF ** -0.5, 0.15625, ((0, 2), (1, 16))),
        "picks": draw_picks(jax.random.fold_in(key_of[6], 71), 0),
        "probe": centred(key_of[5], (SECTIONS, PROJ, D), D ** -0.5, 0.078125, ((0, 2),)),
    }


def rms_rows(rows_in):
    wide = rows_in.astype(jnp.float32)
    scale = lax.rsqrt(lax.optimization_barrier(jnp.mean(wide * wide, axis=-1, keepdims=True)) + 1e-06)
    return (wide * scale).astype(jnp.bfloat16)

def section_step(rows_in, router_s, up_s, down_s, picks_sm):
    normed = rms_rows(rows_in)
    gate_values = jax.nn.sigmoid(jnp.dot(normed, router_s, preferred_element_type=jnp.float32))

    def one_expert(update, expert):
        chosen = picks_sm[expert]
        chosen_rows = jnp.take(normed, chosen, axis=0)
        up_block = lax.dynamic_slice_in_dim(up_s, expert * EXPERT_FF, EXPERT_FF, 0)
        down_block = lax.dynamic_slice_in_dim(down_s, expert * EXPERT_FF, EXPERT_FF, 0)
        pre = lax.dot_general(chosen_rows, up_block, (((1,), (1,)), ((), ())), preferred_element_type=jnp.float32)
        hidden = jax.nn.silu(pre).astype(jnp.bfloat16)
        blocks = jnp.einsum('cki,kid->kcd', hidden.reshape(CAP, SPLIT, FF_DEV).astype(jnp.float32), down_block.reshape(SPLIT, FF_DEV, D).astype(jnp.float32))
        blocks = lax.optimization_barrier(blocks.astype(jnp.bfloat16))
        expert_out = lax.optimization_barrier(jnp.sum(blocks.astype(jnp.float32), axis=0))
        gate_rows = gate_values[chosen, expert]
        update = update.at[chosen].add(gate_rows[:, None] * expert_out)
        return (update, None)
    update, _ = lax.scan(one_expert, jnp.zeros((TOKENS, D), jnp.float32), jnp.arange(EXPERTS, dtype=jnp.int32))
    return (rows_in.astype(jnp.float32) + update).astype(jnp.bfloat16)

def reference(inputs, router, w_up, w_down, picks, probe):
    finals = []
    for micro_index in range(MICRO):
        hidden_rows = inputs[micro_index]
        for section_index in range(SECTIONS):
            hidden_rows = section_step(hidden_rows, router[section_index], w_up[section_index], w_down[section_index], picks[section_index, micro_index])
        finals.append(hidden_rows)
    final = jnp.stack(finals)
    final_normed = rms_rows(final)
    student_rows = jnp.einsum('mtd,pjd->pmtj', final_normed.astype(jnp.float32), probe.astype(jnp.float32))
    return student_rows.astype(jnp.bfloat16)
```

```python
import functools

import jax
import jax.numpy as jnp
from jax import lax
from jax.experimental import pallas as pl
from jax.experimental.pallas import tpu as pltpu
from jax.sharding import PartitionSpec as P

EPS = 1e-06
CUT = 8
MESH = pl.DeviceIdType.MESH
NT = (((1,), (1,)), ((), ()))


def kernel(
    sections, width, experts, x_hbm, router_hbm, up_hbm, down_hbm, picks_hbm, probe_hbm, out_ref,
    x_ref, up_ref, down_ref, probe_ref, lists, place, rows, picked, arrived, partial, returned,
    load_sem, list_send, list_recv, row_send, row_recv, part_send, part_recv,
):
    section = lax.axis_index("pipe")
    me = lax.axis_index("expert")
    tokens, features = x_ref.shape
    hidden_units = up_hbm.shape[0]
    piece = features // CUT
    group = width // experts
    slots = sections * experts
    expert = me // group
    barrier = pltpu.get_barrier_semaphore()

    def greet(step, carry):
        other = lax.rem(me + step, width)
        for far in range(sections):
            to = lax.rem(section + far, sections)
            pl.semaphore_signal(barrier, inc=1, device_id=(to, other), device_id_type=MESH)
        return carry

    for far in range(1, sections):
        to = lax.rem(section + far, sections)
        pl.semaphore_signal(barrier, inc=1, device_id=(to, me), device_id_type=MESH)
    lax.fori_loop(1, width, greet, 0)

    loads = [
        pltpu.make_async_copy(picks_hbm, lists.at[section], load_sem.at[0]),
        pltpu.make_async_copy(x_hbm, x_ref, load_sem.at[1]),
        pltpu.make_async_copy(up_hbm, up_ref.at[pl.ds(0, hidden_units)], load_sem.at[2]),
        pltpu.make_async_copy(
            router_hbm, up_ref.at[pl.ds(hidden_units, router_hbm.shape[0])], load_sem.at[3]
        ),
        pltpu.make_async_copy(down_hbm, down_ref, load_sem.at[4]),
        pltpu.make_async_copy(probe_hbm, probe_ref, load_sem.at[5]),
    ]
    for load in loads:
        load.start()
    loads[0].wait()
    loads[1].wait()

    def places_of(section_lists):
        wide = jnp.concatenate(
            [jnp.broadcast_to(section_lists[e : e + 1], (CUT, section_lists.shape[1]))
             for e in range(experts)], axis=0,
        )
        local = wide - me * tokens
        owned = (local >= 0) & (local < tokens)
        found = jnp.where(owned, local + 1, 0).astype(jnp.float32)
        return jnp.sum(found, axis=1, keepdims=True) - 1.0

    def select(places):
        height = experts * CUT
        token_id = lax.broadcasted_iota(jnp.int32, (height, tokens), 1).astype(jnp.float32)
        cut_id = lax.rem(lax.broadcasted_iota(jnp.int32, (height, tokens), 0), CUT)
        hot = places == token_id
        total = jnp.zeros((height, piece), jnp.float32)
        for c in range(CUT):
            pick = jnp.where(hot & (cut_id == c), 1.0, 0.0).astype(jnp.bfloat16)
            total += jnp.dot(
                pick, x_ref[:, c * piece : (c + 1) * piece], preferred_element_type=jnp.float32
            )
        return total

    def note(which):
        places = places_of(lists[which])
        chosen = select(places)
        first = which * experts
        place[pl.ds(first, experts)] = jnp.broadcast_to(
            places, (experts * CUT, piece)
        ).reshape(experts, CUT, piece)
        rows[pl.ds(first, experts)] = chosen.reshape(experts, CUT, piece)

    note(section)

    def send_rows():
        picked[...] = rows[pl.ds(section * experts, experts)].astype(jnp.bfloat16)

        def send(step, carry):
            other = lax.rem(me + step, width)
            pltpu.make_async_remote_copy(
                src_ref=picked.at[other // group], dst_ref=arrived.at[me], send_sem=row_send,
                recv_sem=row_recv, device_id=(section, other), device_id_type=MESH,
            ).start()
            return carry

        lax.fori_loop(1, width, send, 0)
        pltpu.make_async_copy(picked.at[expert], arrived.at[me], row_recv).start()

    pl.semaphore_wait(barrier, sections * width - 1)

    @pl.when(section == 0)
    def _():
        send_rows()

    def list_copy(far):
        to = lax.rem(section + far, sections)
        return pltpu.make_async_remote_copy(
            src_ref=lists.at[section], dst_ref=lists.at[section], send_sem=list_send.at[far],
            recv_sem=list_recv.at[far], device_id=(to, me), device_id_type=MESH,
        )

    for far in range(1, sections):
        list_copy(far).start()

    loads[5].wait()
    x_all = x_ref[...]
    raw = lax.dot_general(x_all, probe_ref[...], NT, preferred_element_type=jnp.float32)
    x_wide = x_all.astype(jnp.float32)
    square = jnp.sum(x_wide * x_wide, axis=1, keepdims=True)
    base = raw * lax.rsqrt(square * (1.0 / features) + EPS)

    for far in range(1, sections):
        list_copy(far).wait()
        note(lax.rem(section + sections - far, sections))

    loads[2].wait()
    loads[3].wait()
    loads[4].wait()

    def over_cuts(value):
        count, lanes = value.shape
        summed = jnp.sum(value.reshape(count // CUT, CUT, lanes), axis=1, keepdims=True)
        return jnp.broadcast_to(summed, (count // CUT, CUT, lanes)).reshape(count, lanes)

    def expert_block():
        height = width * CUT
        wide = arrived[...].astype(jnp.float32).reshape(height, piece)
        narrow = wide.astype(jnp.bfloat16)
        mean = over_cuts(jnp.sum(wide * wide, axis=1, keepdims=True)) * (1.0 / features)
        scale = lax.rsqrt(mean + EPS)
        columns = up_ref.shape[0]
        cut_up = lax.rem(lax.broadcasted_iota(jnp.int32, (height, columns), 0), CUT)
        pre = jnp.zeros((height, columns), jnp.float32)
        for c in range(CUT):
            term = lax.dot_general(
                narrow, up_ref[:, c * piece : (c + 1) * piece], NT,
                preferred_element_type=jnp.float32,
            )
            pre = jnp.where(cut_up == c, term, pre)
        pre = over_cuts(pre) * scale
        column = lax.broadcasted_iota(jnp.int32, (height, columns), 1)
        logit = jnp.sum(
            jnp.where(column == hidden_units + expert, pre, 0.0), axis=1, keepdims=True
        )
        value = pre[:, :hidden_units]
        gate = 1.0 / (1.0 + jnp.exp(-logit))
        hidden = value / (1.0 + jnp.exp(-value)) * gate
        cut_down = lax.rem(lax.broadcasted_iota(jnp.int32, (height, hidden_units), 0), CUT)
        total = jnp.zeros((height, piece), jnp.float32)
        for c in range(CUT):
            masked = jnp.where(cut_down == c, hidden, 0.0).astype(jnp.bfloat16)
            total += jnp.dot(
                masked, down_ref[:, c * piece : (c + 1) * piece],
                preferred_element_type=jnp.float32,
            )
        partial[...] = total.reshape(width, CUT, piece).astype(jnp.bfloat16)

    def send_parts(phase):
        def give(owner, far):
            to = lax.rem(section + far, sections)
            pltpu.make_async_remote_copy(
                src_ref=partial.at[owner], dst_ref=returned.at[phase, me],
                send_sem=part_send.at[far], recv_sem=part_recv.at[phase],
                device_id=(to, owner), device_id_type=MESH,
            ).start()

        def send(step, carry):
            owner = lax.rem(me + step, width)
            for far in reversed(range(sections)):
                give(owner, far)
            return carry

        lax.fori_loop(1, width, send, 0)
        for far in range(1, sections):
            give(me, far)
        pltpu.make_async_copy(partial.at[me], returned.at[phase, me], part_recv.at[phase]).start()

    def phase_step(phase, carry):
        @pl.when(section == phase)
        def _():
            @pl.when(phase > 0)
            def _():
                send_rows()

            pltpu.make_async_copy(arrived, arrived, row_recv).wait()
            expert_block()
            send_parts(phase)

        pltpu.make_async_copy(returned.at[phase], returned.at[phase], part_recv.at[phase]).wait()
        updates = [
            jnp.sum(
                returned[phase, pl.ds(e * group, group)].astype(jnp.float32), axis=0
            )
            for e in range(experts)
        ]

        def apply(slot, inner):
            total = jnp.zeros((CUT, piece), jnp.float32)
            for e in range(experts):
                same = place[slot] == place[phase * experts + e]
                total += jnp.where(same, updates[e], 0.0)
            rows[slot] = (rows[slot] + total).astype(jnp.bfloat16).astype(jnp.float32)
            return inner

        lax.fori_loop(0, slots, apply, 0, unroll=slots <= 8)
        return carry

    lax.fori_loop(0, sections, phase_step, 0)

    height = slots * CUT
    wide = rows[...].reshape(height, piece)
    mean = over_cuts(jnp.sum(wide * wide, axis=1, keepdims=True)) * (1.0 / features)
    narrow = wide.astype(jnp.bfloat16)
    feats = probe_ref.shape[0]
    cut_out = lax.rem(lax.broadcasted_iota(jnp.int32, (height, feats), 0), CUT)
    changed = jnp.zeros((height, feats), jnp.float32)
    for c in range(CUT):
        term = lax.dot_general(
            narrow, probe_ref[:, c * piece : (c + 1) * piece], NT,
            preferred_element_type=jnp.float32,
        )
        changed = jnp.where(cut_out == c, term, changed)
    changed = over_cuts(changed) * lax.rsqrt(mean + EPS)
    token_id = lax.broadcasted_iota(jnp.int32, (tokens, feats), 0).astype(jnp.float32)
    result = base
    for slot in range(slots):
        at = place[slot][:1, :feats]
        result = jnp.where(token_id == at, changed[slot * CUT : slot * CUT + 1], result)
    out_ref[...] = result.astype(out_ref.dtype)

    for far in range(1, sections):
        pltpu.make_async_copy(returned.at[0], returned.at[0], part_send.at[far]).wait()
    most = returned.at[0, pl.ds(0, width - 1)]
    pltpu.make_async_copy(most, most, part_send.at[0]).wait()
    pltpu.make_async_copy(most, most, row_send).wait()


def shards(inputs, router, w_up, w_down, picks, probe):
    sections = lax.axis_size("pipe")
    width = lax.axis_size("expert")
    tokens, features = inputs.shape[1:]
    experts = router.shape[2]
    cap = picks.shape[3]
    hidden_units = w_up.shape[1]
    feats = probe.shape[1]
    piece = features // CUT
    padded = -(-experts // 16) * 16
    scorer = jnp.pad(jnp.transpose(router[0]), ((0, padded - experts), (0, 0)))
    slots = sections * experts
    any_spec = pl.BlockSpec(memory_space=pl.ANY)
    out = pl.pallas_call(
        functools.partial(kernel, sections, width, experts),
        out_shape=jax.ShapeDtypeStruct((tokens, feats), jnp.bfloat16),
        in_specs=[any_spec] * 6,
        out_specs=pl.BlockSpec(memory_space=pltpu.VMEM),
        scratch_shapes=[
            pltpu.VMEM((tokens, features), jnp.bfloat16),
            pltpu.VMEM((hidden_units + padded, features), jnp.bfloat16),
            pltpu.VMEM((hidden_units, features), jnp.bfloat16),
            pltpu.VMEM((feats, features), jnp.bfloat16),
            pltpu.VMEM((sections, experts, cap), jnp.int32),
            pltpu.VMEM((slots, CUT, piece), jnp.float32),
            pltpu.VMEM((slots, CUT, piece), jnp.float32),
            pltpu.VMEM((experts, CUT, piece), jnp.bfloat16),
            pltpu.VMEM((width, CUT, piece), jnp.bfloat16),
            pltpu.VMEM((width, CUT, piece), jnp.bfloat16),
            pltpu.VMEM((sections, width, CUT, piece), jnp.bfloat16),
            pltpu.SemaphoreType.DMA((6,)),
            pltpu.SemaphoreType.DMA((sections,)),
            pltpu.SemaphoreType.DMA((sections,)),
            pltpu.SemaphoreType.DMA,
            pltpu.SemaphoreType.DMA,
            pltpu.SemaphoreType.DMA((sections,)),
            pltpu.SemaphoreType.DMA((sections,)),
        ],
        compiler_params=pltpu.CompilerParams(collective_id=0, has_side_effects=True),
        name="relay",
    )(inputs[0], scorer, w_up[0], w_down[0], picks[0, 0], probe[0])
    return out[None, None]


def solution(mesh):
    return jax.shard_map(
        shards,
        mesh=mesh,
        in_specs=(
            P(None, "expert", None),
            P("pipe", None, None),
            P("pipe", "expert", None),
            P("pipe", "expert", None),
            P("pipe", None, None, None),
            P("pipe", None, None),
        ),
        out_specs=P("pipe", None, "expert", None),
        check_vma=False,
    )
```

```python
import functools

import jax
import jax.numpy as jnp
from jax import lax
from jax.experimental import pallas as pl
from jax.experimental.pallas import tpu as pltpu
from jax.sharding import PartitionSpec as P

EPS = 1e-06
CUT = 8
PAD = 16
MESH = pl.DeviceIdType.MESH
NT = (((1,), (1,)), ((), ()))


def kernel(
    sections, width, experts, x_hbm, router_hbm, up_hbm, down_hbm, picks_hbm, probe_hbm, out_ref,
    x_ref, up_ref, down_ref, probe_ref, scorer, lists, place, rows, picked, arrived, stage,
    partial, returned, state_out, state_in, load_sem, list_send, list_recv, row_send, row_recv,
    part_send, part_recv, state_send, state_recv,
):
    section = lax.axis_index("pipe")
    me = lax.axis_index("expert")
    tokens, features = x_ref.shape
    hidden_units = up_hbm.shape[0]
    piece = features // CUT
    group = width // experts
    slots = sections * experts
    expert = me // group
    barrier = pltpu.get_barrier_semaphore()

    def around(step):
        index = me + step
        return jnp.where(index >= width, index - width, index)

    def far_pipe(far):
        index = section + far
        return jnp.where(index >= sections, index - sections, index)

    def expert_of(index):
        owner = jnp.int32(0)
        for e in range(1, experts):
            owner = owner + (index >= e * group).astype(jnp.int32)
        return owner

    steps = sorted(range(1, width), key=lambda step: -min(step, width - step))

    def each_step(act):
        if width <= 16:
            for step in steps:
                act(step)
        else:
            lax.fori_loop(1, width, lambda step, carry: (act(step), carry)[1], 0)

    def greet(step):
        other = around(step)
        for far in range(sections):
            to = far_pipe(far)
            pl.semaphore_signal(barrier, inc=1, device_id=(to, other), device_id_type=MESH)

    for far in range(1, sections):
        to = far_pipe(far)
        pl.semaphore_signal(barrier, inc=1, device_id=(to, me), device_id_type=MESH)
    each_step(greet)

    loads = [
        pltpu.make_async_copy(picks_hbm, lists.at[section], load_sem.at[0]),
        pltpu.make_async_copy(x_hbm, x_ref, load_sem.at[1]),
        pltpu.make_async_copy(up_hbm, up_ref.at[pl.ds(0, hidden_units)], load_sem.at[2]),
        pltpu.make_async_copy(router_hbm, scorer, load_sem.at[3]),
        pltpu.make_async_copy(down_hbm, down_ref, load_sem.at[4]),
        pltpu.make_async_copy(probe_hbm, probe_ref, load_sem.at[5]),
    ]
    for load in loads:
        load.start()
    loads[0].wait()
    loads[1].wait()

    def places_of(section_lists):
        wide = jnp.concatenate(
            [jnp.broadcast_to(section_lists[e : e + 1], (CUT, section_lists.shape[1]))
             for e in range(experts)], axis=0,
        )
        local = wide - me * tokens
        owned = (local >= 0) & (local < tokens)
        found = jnp.where(owned, local + 1, 0).astype(jnp.float32)
        return jnp.sum(found, axis=1, keepdims=True) - 1.0

    def select(places):
        height = experts * CUT
        token_id = lax.broadcasted_iota(jnp.int32, (height, tokens), 1).astype(jnp.float32)
        cut_id = lax.rem(lax.broadcasted_iota(jnp.int32, (height, tokens), 0), CUT)
        hot = places == token_id
        total = jnp.zeros((height, piece), jnp.float32)
        for c in range(CUT):
            pick = jnp.where(hot & (cut_id == c), 1.0, 0.0).astype(jnp.bfloat16)
            total += jnp.dot(
                pick, x_ref[:, c * piece : (c + 1) * piece], preferred_element_type=jnp.float32
            )
        return total

    def note(which):
        places = places_of(lists[which])
        chosen = select(places)
        first = which * experts
        place[pl.ds(first, experts)] = jnp.broadcast_to(
            places, (experts * CUT, piece)
        ).reshape(experts, CUT, piece)
        rows[pl.ds(first, experts)] = chosen.reshape(experts, CUT, piece)

    note(section)

    def send_rows():
        picked[...] = rows[pl.ds(section * experts, experts)].astype(jnp.bfloat16)

        def send(step):
            other = around(step)
            pltpu.make_async_remote_copy(
                src_ref=picked.at[expert_of(other)], dst_ref=arrived.at[me], send_sem=row_send,
                recv_sem=row_recv, device_id=(section, other), device_id_type=MESH,
            ).start()

        each_step(send)
        pltpu.make_async_copy(picked.at[expert], arrived.at[me], row_recv).start()

    pl.semaphore_wait(barrier, sections * width - 1)

    @pl.when(section == 0)
    def _():
        send_rows()

    def list_copy(far):
        to = far_pipe(far)
        return pltpu.make_async_remote_copy(
            src_ref=lists.at[section], dst_ref=lists.at[section], send_sem=list_send.at[far],
            recv_sem=list_recv.at[far], device_id=(to, me), device_id_type=MESH,
        )

    for far in range(1, sections):
        list_copy(far).start()

    loads[5].wait()
    x_all = x_ref[...]
    raw = lax.dot_general(x_all, probe_ref[...], NT, preferred_element_type=jnp.float32)
    x_wide = x_all.astype(jnp.float32)
    square = jnp.sum(x_wide * x_wide, axis=1, keepdims=True)
    base = raw * lax.rsqrt(square * (1.0 / features) + EPS)

    for far in range(1, sections):
        list_copy(far).wait()
        note(lax.rem(section + sections - far, sections))

    loads[2].wait()
    loads[3].wait()
    up_ref[pl.ds(hidden_units, PAD)] = jnp.zeros((PAD, features), jnp.bfloat16)
    up_ref[pl.ds(hidden_units, experts)] = scorer[...]
    loads[4].wait()

    def over_cuts(value):
        count, lanes = value.shape
        summed = jnp.sum(value.reshape(count // CUT, CUT, lanes), axis=1, keepdims=True)
        return jnp.broadcast_to(summed, (count // CUT, CUT, lanes)).reshape(count, lanes)

    def expert_block():
        wide = arrived[...].astype(jnp.float32).reshape(width * CUT, piece)
        lanes = stage.shape[2]
        for t in range(piece // lanes):
            stage[t] = wide[:, t * lanes : (t + 1) * lanes]
        squares = jnp.sum((wide * wide).reshape(width, CUT, piece), axis=1)
        scale = lax.rsqrt(jnp.sum(squares, axis=1, keepdims=True) * (1.0 / features) + EPS)
        columns = up_ref.shape[0]
        pre = jnp.zeros((width, columns), jnp.float32)
        for c in range(CUT):
            pre += lax.dot_general(
                jnp.concatenate(
                    [stage[t, pl.ds(c, width, stride=CUT)] for t in range(piece // lanes)], axis=1
                ).astype(jnp.bfloat16),
                up_ref[:, c * piece : (c + 1) * piece], NT,
                preferred_element_type=jnp.float32,
            )
        pre = pre * scale
        column = lax.broadcasted_iota(jnp.int32, (width, columns), 1)
        logit = jnp.sum(
            jnp.where(column == hidden_units + expert, pre, 0.0), axis=1, keepdims=True
        )
        value = pre[:, :hidden_units]
        gate = 1.0 / (1.0 + jnp.exp(-logit))
        hidden = (value / (1.0 + jnp.exp(-value)) * gate).astype(jnp.bfloat16)
        for c in range(CUT):
            block = jnp.dot(
                hidden, down_ref[:, c * piece : (c + 1) * piece],
                preferred_element_type=jnp.float32,
            )
            for t in range(piece // lanes):
                stage[t, pl.ds(c, width, stride=CUT)] = block[:, t * lanes : (t + 1) * lanes]
        for t in range(piece // lanes):
            partial[:, :, t * lanes : (t + 1) * lanes] = (
                stage[t].reshape(width, CUT, lanes).astype(jnp.bfloat16)
            )

    def give(owner, far, batch):
        pltpu.make_async_remote_copy(
            src_ref=partial.at[owner], dst_ref=returned.at[batch, me],
            send_sem=part_send.at[far], recv_sem=part_recv.at[batch],
            device_id=(far_pipe(far), owner), device_id_type=MESH,
        ).start()

    def pass_parts():
        each_step(lambda step: give(around(step), 1, 0))
        give(me, 1, 0)

    def share_parts():
        def send(step):
            for far in reversed(range(sections)):
                give(around(step), far, 1)

        each_step(send)
        for far in range(1, sections):
            give(me, far, 1)
        pltpu.make_async_copy(partial.at[me], returned.at[1, me], part_recv.at[1]).start()

    def give_state(far, batch):
        return pltpu.make_async_remote_copy(
            src_ref=state_out, dst_ref=state_in.at[batch], send_sem=state_send.at[far],
            recv_sem=state_recv.at[batch], device_id=(far_pipe(far), me), device_id_type=MESH,
        )

    def take_state(batch):
        pltpu.make_async_copy(state_in.at[batch], state_in.at[batch], state_recv.at[batch]).wait()
        rows[...] = state_in[batch].astype(jnp.float32)

    def take_parts(phase, batch):
        pltpu.make_async_copy(returned.at[batch], returned.at[batch], part_recv.at[batch]).wait()
        updates = [
            jnp.sum(returned[batch, pl.ds(e * group, group)].astype(jnp.float32), axis=0)
            for e in range(experts)
        ]

        def apply(slot, carry):
            total = jnp.zeros((CUT, piece), jnp.float32)
            for e in range(experts):
                same = place[slot] == place[phase * experts + e]
                total += jnp.where(same, updates[e], 0.0)
            rows[slot] = (rows[slot] + total).astype(jnp.bfloat16).astype(jnp.float32)
            return carry

        lax.fori_loop(0, slots, apply, 0, unroll=slots <= 8)

    last = sections - 1

    @pl.when(section < last)
    def _():
        @pl.when(section > 0)
        def _():
            @pl.when(section > 1)
            def _():
                take_state(0)

            take_parts(section - 1, 0)
            send_rows()
            state_out[...] = rows[...].astype(jnp.bfloat16)
            give_state(1, 0).start()

        pltpu.make_async_copy(arrived, arrived, row_recv).wait()
        expert_block()
        pass_parts()

    @pl.when(section == last)
    def _():
        if last > 0:
            if last > 1:
                take_state(0)
            take_parts(section - 1, 0)
            send_rows()
            state_out[...] = rows[...].astype(jnp.bfloat16)
            for far in range(1, sections):
                give_state(far, 1).start()
        pltpu.make_async_copy(arrived, arrived, row_recv).wait()
        expert_block()
        share_parts()

    if last > 0:
        @pl.when(section < last)
        def _():
            take_state(1)

    take_parts(last, 1)

    height = slots * CUT
    wide = rows[...].reshape(height, piece)
    mean = over_cuts(jnp.sum(wide * wide, axis=1, keepdims=True)) * (1.0 / features)
    narrow = wide.astype(jnp.bfloat16)
    feats = probe_ref.shape[0]
    cut_out = lax.rem(lax.broadcasted_iota(jnp.int32, (height, feats), 0), CUT)
    changed = jnp.zeros((height, feats), jnp.float32)
    for c in range(CUT):
        term = lax.dot_general(
            narrow, probe_ref[:, c * piece : (c + 1) * piece], NT,
            preferred_element_type=jnp.float32,
        )
        changed = jnp.where(cut_out == c, term, changed)
    changed = over_cuts(changed) * lax.rsqrt(mean + EPS)
    token_id = lax.broadcasted_iota(jnp.int32, (tokens, feats), 0).astype(jnp.float32)
    result = base
    for slot in range(slots):
        at = place[slot][:1, :feats]
        result = jnp.where(token_id == at, changed[slot * CUT : slot * CUT + 1], result)
    out_ref[...] = result.astype(out_ref.dtype)

    most = returned.at[0, pl.ds(0, width - 1)]
    pltpu.make_async_copy(most, most, row_send).wait()

    @pl.when(section < last)
    def _():
        pltpu.make_async_copy(returned.at[0], returned.at[0], part_send.at[1 % sections]).wait()

        @pl.when(section > 0)
        def _():
            give_state(1, 0).wait_send()

    @pl.when(section == last)
    def _():
        pltpu.make_async_copy(most, most, part_send.at[0]).wait()
        for far in range(1, sections):
            pltpu.make_async_copy(returned.at[0], returned.at[0], part_send.at[far]).wait()
            give_state(far, 1).wait_send()


def shards(inputs, router, w_up, w_down, picks, probe):
    sections = lax.axis_size("pipe")
    width = lax.axis_size("expert")
    tokens, features = inputs.shape[1:]
    experts = router.shape[2]
    cap = picks.shape[3]
    hidden_units = w_up.shape[1]
    feats = probe.shape[1]
    piece = features // CUT
    slots = sections * experts
    any_spec = pl.BlockSpec(memory_space=pl.ANY)
    out = pl.pallas_call(
        functools.partial(kernel, sections, width, experts),
        out_shape=jax.ShapeDtypeStruct((tokens, feats), jnp.bfloat16),
        in_specs=[any_spec] * 6,
        out_specs=pl.BlockSpec(memory_space=pltpu.VMEM),
        scratch_shapes=[
            pltpu.VMEM((tokens, features), jnp.bfloat16),
            pltpu.VMEM((hidden_units + PAD, features), jnp.bfloat16),
            pltpu.VMEM((hidden_units, features), jnp.bfloat16),
            pltpu.VMEM((feats, features), jnp.bfloat16),
            pltpu.VMEM((experts, features), jnp.bfloat16),
            pltpu.VMEM((sections, experts, cap), jnp.int32),
            pltpu.VMEM((slots, CUT, piece), jnp.float32),
            pltpu.VMEM((slots, CUT, piece), jnp.float32),
            pltpu.VMEM((experts, CUT, piece), jnp.bfloat16),
            pltpu.VMEM((width, CUT, piece), jnp.bfloat16),
            pltpu.VMEM((piece // 128, width * CUT, 128), jnp.float32),
            pltpu.VMEM((width, CUT, piece), jnp.bfloat16),
            pltpu.VMEM((2, width, CUT, piece), jnp.bfloat16),
            pltpu.VMEM((slots, CUT, piece), jnp.bfloat16),
            pltpu.VMEM((2, slots, CUT, piece), jnp.bfloat16),
            pltpu.SemaphoreType.DMA((6,)),
            pltpu.SemaphoreType.DMA((sections,)),
            pltpu.SemaphoreType.DMA((sections,)),
            pltpu.SemaphoreType.DMA,
            pltpu.SemaphoreType.DMA,
            pltpu.SemaphoreType.DMA((sections,)),
            pltpu.SemaphoreType.DMA((2,)),
            pltpu.SemaphoreType.DMA((sections,)),
            pltpu.SemaphoreType.DMA((2,)),
        ],
        compiler_params=pltpu.CompilerParams(collective_id=0, has_side_effects=True),
        name="relay",
    )(inputs[0], jnp.transpose(router[0]), w_up[0], w_down[0], picks[0, 0], probe[0])
    return out[None, None]


def solution(mesh):
    return jax.shard_map(
        shards,
        mesh=mesh,
        in_specs=(
            P(None, "expert", None),
            P("pipe", None, None),
            P("pipe", "expert", None),
            P("pipe", "expert", None),
            P("pipe", None, None, None),
            P("pipe", None, None),
        ),
        out_specs=P("pipe", None, "expert", None),
        check_vma=False,
    )
```

```python
import functools

import jax
import jax.numpy as jnp
from jax import lax
from jax.experimental import pallas as pl
from jax.experimental.pallas import tpu as pltpu
from jax.sharding import PartitionSpec as P

EPS = 1e-06
CUT = 8
PAD = 16
JOIN = 2
MESH = pl.DeviceIdType.MESH
NT = (((1,), (1,)), ((), ()))


def kernel(
    sections, width, experts, x_hbm, router_hbm, up_hbm, down_hbm, picks_hbm, probe_hbm, out_ref,
    x_ref, up_ref, down_ref, probe_ref, scorer, lists, place, rows, picked, arrived, stage,
    partial, returned, state_out, state_in, load_sem, list_send, list_recv, row_send, row_recv,
    part_send, part_recv, state_send, state_recv,
):
    section = lax.axis_index("pipe")
    me = lax.axis_index("expert")
    tokens, features = x_ref.shape
    hidden_units = up_hbm.shape[0]
    piece = features // CUT
    group = width // experts
    slots = sections * experts
    expert = me // group
    barrier = pltpu.get_barrier_semaphore()

    def around(step):
        index = me + step
        return jnp.where(index >= width, index - width, index)

    def far_pipe(far):
        index = section + far
        return jnp.where(index >= sections, index - sections, index)

    def expert_of(index):
        owner = jnp.int32(0)
        for e in range(1, experts):
            owner = owner + (index >= e * group).astype(jnp.int32)
        return owner

    steps = range(1, width)

    def each_step(act):
        if width <= 16:
            for step in steps:
                act(step)
        else:
            lax.fori_loop(1, width, lambda step, carry: (act(step), carry)[1], 0)

    def greet(step):
        other = around(step)
        for far in range(sections):
            to = far_pipe(far)
            pl.semaphore_signal(barrier, inc=1, device_id=(to, other), device_id_type=MESH)

    for far in range(1, sections):
        to = far_pipe(far)
        pl.semaphore_signal(barrier, inc=1, device_id=(to, me), device_id_type=MESH)
    each_step(greet)

    loads = [
        pltpu.make_async_copy(picks_hbm, lists.at[section], load_sem.at[0]),
        pltpu.make_async_copy(x_hbm, x_ref, load_sem.at[1]),
        pltpu.make_async_copy(up_hbm, up_ref.at[pl.ds(0, hidden_units)], load_sem.at[2]),
        pltpu.make_async_copy(router_hbm, scorer, load_sem.at[3]),
        pltpu.make_async_copy(down_hbm, down_ref, load_sem.at[4]),
        pltpu.make_async_copy(probe_hbm, probe_ref, load_sem.at[5]),
    ]
    for load in loads:
        load.start()
    loads[0].wait()
    loads[1].wait()

    def places_of(section_lists):
        wide = jnp.concatenate(
            [jnp.broadcast_to(section_lists[e : e + 1], (CUT, section_lists.shape[1]))
             for e in range(experts)], axis=0,
        )
        local = wide - me * tokens
        owned = (local >= 0) & (local < tokens)
        found = jnp.where(owned, local + 1, 0).astype(jnp.float32)
        return jnp.sum(found, axis=1, keepdims=True) - 1.0

    def select(places):
        height = experts * CUT
        token_id = lax.broadcasted_iota(jnp.int32, (height, tokens), 1).astype(jnp.float32)
        cut_id = lax.rem(lax.broadcasted_iota(jnp.int32, (height, tokens), 0), CUT)
        hot = places == token_id
        total = jnp.zeros((height, piece), jnp.float32)
        for c in range(CUT):
            pick = jnp.where(hot & (cut_id == c), 1.0, 0.0).astype(jnp.bfloat16)
            total += jnp.dot(
                pick, x_ref[:, c * piece : (c + 1) * piece], preferred_element_type=jnp.float32
            )
        return total

    def note(which):
        places = places_of(lists[which])
        chosen = select(places)
        first = which * experts
        place[pl.ds(first, experts)] = jnp.broadcast_to(
            places, (experts * CUT, piece)
        ).reshape(experts, CUT, piece)
        rows[pl.ds(first, experts)] = chosen.reshape(experts, CUT, piece)

    note(section)

    def send_rows():
        picked[...] = rows[pl.ds(section * experts, experts)].astype(jnp.bfloat16)

        def send(step):
            other = around(step)
            pltpu.make_async_remote_copy(
                src_ref=picked.at[expert_of(other)], dst_ref=arrived.at[me], send_sem=row_send,
                recv_sem=row_recv, device_id=(section, other), device_id_type=MESH,
            ).start()

        each_step(send)
        pltpu.make_async_copy(picked.at[expert], arrived.at[me], row_recv).start()

    pl.semaphore_wait(barrier, sections * width - 1)

    @pl.when(section == 0)
    def _():
        send_rows()

    def list_copy(far):
        to = far_pipe(far)
        return pltpu.make_async_remote_copy(
            src_ref=lists.at[section], dst_ref=lists.at[section], send_sem=list_send.at[far],
            recv_sem=list_recv.at[far], device_id=(to, me), device_id_type=MESH,
        )

    for far in range(1, sections):
        list_copy(far).start()

    loads[5].wait()
    x_all = x_ref[...]
    raw = lax.dot_general(x_all, probe_ref[...], NT, preferred_element_type=jnp.float32)
    x_wide = x_all.astype(jnp.float32)
    square = jnp.sum(x_wide * x_wide, axis=1, keepdims=True)
    base = raw * lax.rsqrt(square * (1.0 / features) + EPS)

    for far in range(1, sections):
        list_copy(far).wait()
        note(lax.rem(section + sections - far, sections))

    loads[2].wait()
    loads[3].wait()
    up_ref[pl.ds(hidden_units, PAD)] = jnp.zeros((PAD, features), jnp.bfloat16)
    up_ref[pl.ds(hidden_units, experts)] = scorer[...]
    loads[4].wait()

    def over_cuts(value):
        count, lanes = value.shape
        summed = jnp.sum(value.reshape(count // CUT, CUT, lanes), axis=1, keepdims=True)
        return jnp.broadcast_to(summed, (count // CUT, CUT, lanes)).reshape(count, lanes)

    def expert_block():
        wide = arrived[...].astype(jnp.float32).reshape(width * CUT, piece)
        lanes = stage.shape[2]
        for t in range(piece // lanes):
            stage[t] = wide[:, t * lanes : (t + 1) * lanes]
        squares = jnp.sum((wide * wide).reshape(width, CUT, piece), axis=1)
        scale = lax.rsqrt(jnp.sum(squares, axis=1, keepdims=True) * (1.0 / features) + EPS)
        columns = up_ref.shape[0]
        pre = jnp.zeros((width, columns), jnp.float32)
        for c in range(0, CUT, JOIN):
            pre += lax.dot_general(
                jnp.concatenate(
                    [stage[t, pl.ds(c + i, width, stride=CUT)]
                     for i in range(JOIN) for t in range(piece // lanes)], axis=1
                ).astype(jnp.bfloat16),
                up_ref[:, c * piece : (c + JOIN) * piece], NT,
                preferred_element_type=jnp.float32,
            )
        pre = pre * scale
        column = lax.broadcasted_iota(jnp.int32, (width, columns), 1)
        logit = jnp.sum(
            jnp.where(column == hidden_units + expert, pre, 0.0), axis=1, keepdims=True
        )
        value = pre[:, :hidden_units]
        gate = 1.0 / (1.0 + jnp.exp(-logit))
        hidden = (value / (1.0 + jnp.exp(-value)) * gate).astype(jnp.bfloat16)
        for c in range(0, CUT, JOIN):
            block = jnp.dot(
                hidden, down_ref[:, c * piece : (c + JOIN) * piece],
                preferred_element_type=jnp.float32,
            )
            for i in range(JOIN):
                for t in range(piece // lanes):
                    at = i * piece + t * lanes
                    stage[t, pl.ds(c + i, width, stride=CUT)] = block[:, at : at + lanes]
        for t in range(piece // lanes):
            partial[:, :, t * lanes : (t + 1) * lanes] = (
                stage[t].reshape(width, CUT, lanes).astype(jnp.bfloat16)
            )

    def give(owner, far, batch):
        pltpu.make_async_remote_copy(
            src_ref=partial.at[owner], dst_ref=returned.at[batch, me],
            send_sem=part_send.at[far], recv_sem=part_recv.at[batch],
            device_id=(far_pipe(far), owner), device_id_type=MESH,
        ).start()

    def pass_parts():
        each_step(lambda step: give(around(step), 1, 0))
        give(me, 1, 0)

    def share_parts():
        def send(step):
            for far in reversed(range(sections)):
                give(around(step), far, 1)

        each_step(send)
        for far in range(1, sections):
            give(me, far, 1)
        pltpu.make_async_copy(partial.at[me], returned.at[1, me], part_recv.at[1]).start()

    def give_state(far, batch):
        return pltpu.make_async_remote_copy(
            src_ref=state_out, dst_ref=state_in.at[batch], send_sem=state_send.at[far],
            recv_sem=state_recv.at[batch], device_id=(far_pipe(far), me), device_id_type=MESH,
        )

    def take_state(batch):
        pltpu.make_async_copy(state_in.at[batch], state_in.at[batch], state_recv.at[batch]).wait()
        rows[...] = state_in[batch].astype(jnp.float32)

    def take_parts(phase, batch):
        pltpu.make_async_copy(returned.at[batch], returned.at[batch], part_recv.at[batch]).wait()
        updates = [
            jnp.sum(returned[batch, pl.ds(e * group, group)].astype(jnp.float32), axis=0)
            for e in range(experts)
        ]

        def apply(slot, carry):
            total = jnp.zeros((CUT, piece), jnp.float32)
            for e in range(experts):
                same = place[slot] == place[phase * experts + e]
                total += jnp.where(same, updates[e], 0.0)
            rows[slot] = (rows[slot] + total).astype(jnp.bfloat16).astype(jnp.float32)
            return carry

        lax.fori_loop(0, slots, apply, 0, unroll=slots <= 8)

    last = sections - 1

    @pl.when(section < last)
    def _():
        @pl.when(section > 0)
        def _():
            @pl.when(section > 1)
            def _():
                take_state(0)

            take_parts(section - 1, 0)
            send_rows()
            state_out[...] = rows[...].astype(jnp.bfloat16)
            give_state(1, 0).start()

        pltpu.make_async_copy(arrived, arrived, row_recv).wait()
        expert_block()
        pass_parts()

    @pl.when(section == last)
    def _():
        if last > 0:
            if last > 1:
                take_state(0)
            take_parts(section - 1, 0)
            send_rows()
            state_out[...] = rows[...].astype(jnp.bfloat16)
            for far in range(1, sections):
                give_state(far, 1).start()
        pltpu.make_async_copy(arrived, arrived, row_recv).wait()
        expert_block()
        share_parts()

    if last > 0:
        @pl.when(section < last)
        def _():
            take_state(1)

    take_parts(last, 1)

    height = slots * CUT
    wide = rows[...].reshape(height, piece)
    mean = over_cuts(jnp.sum(wide * wide, axis=1, keepdims=True)) * (1.0 / features)
    narrow = wide.astype(jnp.bfloat16)
    feats = probe_ref.shape[0]
    cut_out = lax.rem(lax.broadcasted_iota(jnp.int32, (height, feats), 0), CUT)
    changed = jnp.zeros((height, feats), jnp.float32)
    for c in range(CUT):
        term = lax.dot_general(
            narrow, probe_ref[:, c * piece : (c + 1) * piece], NT,
            preferred_element_type=jnp.float32,
        )
        changed = jnp.where(cut_out == c, term, changed)
    changed = over_cuts(changed) * lax.rsqrt(mean + EPS)
    token_id = lax.broadcasted_iota(jnp.int32, (tokens, feats), 0).astype(jnp.float32)
    result = base
    for slot in range(slots):
        at = place[slot][:1, :feats]
        result = jnp.where(token_id == at, changed[slot * CUT : slot * CUT + 1], result)
    out_ref[...] = result.astype(out_ref.dtype)

    most = returned.at[0, pl.ds(0, width - 1)]
    pltpu.make_async_copy(most, most, row_send).wait()

    @pl.when(section < last)
    def _():
        pltpu.make_async_copy(returned.at[0], returned.at[0], part_send.at[1 % sections]).wait()

        @pl.when(section > 0)
        def _():
            give_state(1, 0).wait_send()

    @pl.when(section == last)
    def _():
        pltpu.make_async_copy(most, most, part_send.at[0]).wait()
        for far in range(1, sections):
            pltpu.make_async_copy(returned.at[0], returned.at[0], part_send.at[far]).wait()
            give_state(far, 1).wait_send()


def shards(inputs, router, w_up, w_down, picks, probe):
    sections = lax.axis_size("pipe")
    width = lax.axis_size("expert")
    tokens, features = inputs.shape[1:]
    experts = router.shape[2]
    cap = picks.shape[3]
    hidden_units = w_up.shape[1]
    feats = probe.shape[1]
    piece = features // CUT
    slots = sections * experts
    any_spec = pl.BlockSpec(memory_space=pl.ANY)
    out = pl.pallas_call(
        functools.partial(kernel, sections, width, experts),
        out_shape=jax.ShapeDtypeStruct((tokens, feats), jnp.bfloat16),
        in_specs=[any_spec] * 6,
        out_specs=pl.BlockSpec(memory_space=pltpu.VMEM),
        scratch_shapes=[
            pltpu.VMEM((tokens, features), jnp.bfloat16),
            pltpu.VMEM((hidden_units + PAD, features), jnp.bfloat16),
            pltpu.VMEM((hidden_units, features), jnp.bfloat16),
            pltpu.VMEM((feats, features), jnp.bfloat16),
            pltpu.VMEM((experts, features), jnp.bfloat16),
            pltpu.VMEM((sections, experts, cap), jnp.int32),
            pltpu.VMEM((slots, CUT, piece), jnp.float32),
            pltpu.VMEM((slots, CUT, piece), jnp.float32),
            pltpu.VMEM((experts, CUT, piece), jnp.bfloat16),
            pltpu.VMEM((width, CUT, piece), jnp.bfloat16),
            pltpu.VMEM((piece // 128, width * CUT, 128), jnp.float32),
            pltpu.VMEM((width, CUT, piece), jnp.bfloat16),
            pltpu.VMEM((2, width, CUT, piece), jnp.bfloat16),
            pltpu.VMEM((slots, CUT, piece), jnp.bfloat16),
            pltpu.VMEM((2, slots, CUT, piece), jnp.bfloat16),
            pltpu.SemaphoreType.DMA((6,)),
            pltpu.SemaphoreType.DMA((sections,)),
            pltpu.SemaphoreType.DMA((sections,)),
            pltpu.SemaphoreType.DMA,
            pltpu.SemaphoreType.DMA,
            pltpu.SemaphoreType.DMA((sections,)),
            pltpu.SemaphoreType.DMA((2,)),
            pltpu.SemaphoreType.DMA((sections,)),
            pltpu.SemaphoreType.DMA((2,)),
        ],
        compiler_params=pltpu.CompilerParams(collective_id=0, has_side_effects=True),
        name="relay",
    )(inputs[0], jnp.transpose(router[0]), w_up[0], w_down[0], picks[0, 0], probe[0])
    return out[None, None]


def solution(mesh):
    return jax.shard_map(
        shards,
        mesh=mesh,
        in_specs=(
            P(None, "expert", None),
            P("pipe", None, None),
            P("pipe", "expert", None),
            P("pipe", "expert", None),
            P("pipe", None, None, None),
            P("pipe", None, None),
        ),
        out_specs=P("pipe", None, "expert", None),
        check_vma=False,
    )
```

```python
import functools

import jax
import jax.numpy as jnp
from jax import lax
from jax.experimental import pallas as pl
from jax.experimental.pallas import tpu as pltpu
from jax.sharding import PartitionSpec as P

EPS = 1e-06
CUT = 8
PAD = 16
JOIN = 2
MESH = pl.DeviceIdType.MESH
NT = (((1,), (1,)), ((), ()))


def kernel(
    sections, width, experts, x_hbm, router_hbm, up_hbm, down_hbm, picks_hbm, probe_hbm, out_ref,
    x_ref, up_ref, down_ref, probe_ref, scorer, lists, place, rows, picked, arrived, stage,
    partial, returned, state_out, state_in, load_sem, list_send, list_recv, row_send, row_recv,
    part_send, part_recv, state_send, state_recv,
):
    section = lax.axis_index("pipe")
    me = lax.axis_index("expert")
    tokens, features = x_ref.shape
    hidden_units = up_hbm.shape[0]
    piece = features // CUT
    group = width // experts
    slots = sections * experts
    expert = me // group
    barrier = pltpu.get_barrier_semaphore()

    def around(step):
        index = me + step
        return jnp.where(index >= width, index - width, index)

    def far_pipe(far):
        index = section + far
        return jnp.where(index >= sections, index - sections, index)

    def expert_of(index):
        owner = jnp.int32(0)
        for e in range(1, experts):
            owner = owner + (index >= e * group).astype(jnp.int32)
        return owner

    steps = range(1, width)

    def each_step(act):
        if width <= 16:
            for step in steps:
                act(step)
        else:
            lax.fori_loop(1, width, lambda step, carry: (act(step), carry)[1], 0)

    def greet(step):
        other = around(step)
        for far in range(sections):
            to = far_pipe(far)
            pl.semaphore_signal(barrier, inc=1, device_id=(to, other), device_id_type=MESH)

    for far in range(1, sections):
        to = far_pipe(far)
        pl.semaphore_signal(barrier, inc=1, device_id=(to, me), device_id_type=MESH)
    each_step(greet)

    loads = [
        pltpu.make_async_copy(picks_hbm, lists.at[section], load_sem.at[0]),
        pltpu.make_async_copy(x_hbm, x_ref, load_sem.at[1]),
        pltpu.make_async_copy(up_hbm, up_ref.at[pl.ds(0, hidden_units)], load_sem.at[2]),
        pltpu.make_async_copy(router_hbm, scorer, load_sem.at[3]),
        pltpu.make_async_copy(down_hbm, down_ref, load_sem.at[4]),
        pltpu.make_async_copy(probe_hbm, probe_ref, load_sem.at[5]),
    ]
    for load in loads:
        load.start()
    loads[0].wait()
    loads[1].wait()

    def places_of(section_lists):
        wide = jnp.concatenate(
            [jnp.broadcast_to(section_lists[e : e + 1], (CUT, section_lists.shape[1]))
             for e in range(experts)], axis=0,
        )
        local = wide - me * tokens
        owned = (local >= 0) & (local < tokens)
        found = jnp.where(owned, local + 1, 0).astype(jnp.float32)
        return jnp.sum(found, axis=1, keepdims=True) - 1.0

    def select(places):
        height = experts * CUT
        token_id = lax.broadcasted_iota(jnp.int32, (height, tokens), 1).astype(jnp.float32)
        cut_id = lax.rem(lax.broadcasted_iota(jnp.int32, (height, tokens), 0), CUT)
        hot = places == token_id
        total = jnp.zeros((height, piece), jnp.float32)
        for c in range(CUT):
            pick = jnp.where(hot & (cut_id == c), 1.0, 0.0).astype(jnp.bfloat16)
            total += jnp.dot(
                pick, x_ref[:, c * piece : (c + 1) * piece], preferred_element_type=jnp.float32
            )
        return total

    def note(which):
        places = places_of(lists[which])
        chosen = select(places)
        first = which * experts
        place[pl.ds(first, experts)] = jnp.broadcast_to(
            places, (experts * CUT, piece)
        ).reshape(experts, CUT, piece)
        rows[pl.ds(first, experts)] = chosen.reshape(experts, CUT, piece)

    note(section)

    def send_rows():
        picked[...] = rows[pl.ds(section * experts, experts)].astype(jnp.bfloat16)

        def send(step):
            other = around(step)
            pltpu.make_async_remote_copy(
                src_ref=picked.at[expert_of(other)], dst_ref=arrived.at[me], send_sem=row_send,
                recv_sem=row_recv, device_id=(section, other), device_id_type=MESH,
            ).start()

        each_step(send)
        pltpu.make_async_copy(picked.at[expert], arrived.at[me], row_recv).start()

    pl.semaphore_wait(barrier, sections * width - 1)

    @pl.when(section == 0)
    def _():
        send_rows()

    def list_copy(far):
        to = far_pipe(far)
        return pltpu.make_async_remote_copy(
            src_ref=lists.at[section], dst_ref=lists.at[section], send_sem=list_send.at[far],
            recv_sem=list_recv.at[far], device_id=(to, me), device_id_type=MESH,
        )

    for far in range(1, sections):
        list_copy(far).start()

    loads[5].wait()
    x_all = x_ref[...]
    raw = lax.dot_general(x_all, probe_ref[...], NT, preferred_element_type=jnp.float32)
    x_wide = x_all.astype(jnp.float32)
    square = jnp.sum(x_wide * x_wide, axis=1, keepdims=True)
    base = raw * lax.rsqrt(square * (1.0 / features) + EPS)

    for far in range(1, sections):
        list_copy(far).wait()
        note(lax.rem(section + sections - far, sections))

    loads[2].wait()
    loads[3].wait()
    up_ref[pl.ds(hidden_units, PAD)] = jnp.zeros((PAD, features), jnp.bfloat16)
    up_ref[pl.ds(hidden_units, experts)] = scorer[...]
    loads[4].wait()

    def over_cuts(value):
        count, lanes = value.shape
        summed = jnp.sum(value.reshape(count // CUT, CUT, lanes), axis=1, keepdims=True)
        return jnp.broadcast_to(summed, (count // CUT, CUT, lanes)).reshape(count, lanes)

    def expert_block():
        wide = arrived[...].astype(jnp.float32).reshape(width * CUT, piece)
        lanes = stage.shape[2]
        for t in range(piece // lanes):
            stage[t] = wide[:, t * lanes : (t + 1) * lanes]
        squares = jnp.sum((wide * wide).reshape(width, CUT, piece), axis=1)
        scale = lax.rsqrt(jnp.sum(squares, axis=1, keepdims=True) * (1.0 / features) + EPS)
        columns = up_ref.shape[0]
        pre = jnp.zeros((width, columns), jnp.float32)
        for c in range(0, CUT, JOIN):
            pre += lax.dot_general(
                jnp.concatenate(
                    [stage[t, pl.ds(c + i, width, stride=CUT)]
                     for i in range(JOIN) for t in range(piece // lanes)], axis=1
                ).astype(jnp.bfloat16),
                up_ref[:, c * piece : (c + JOIN) * piece], NT,
                preferred_element_type=jnp.float32,
            )
        pre = pre * scale
        column = lax.broadcasted_iota(jnp.int32, (width, columns), 1)
        logit = jnp.sum(
            jnp.where(column == hidden_units + expert, pre, 0.0), axis=1, keepdims=True
        )
        value = pre[:, :hidden_units]
        gate = 1.0 / (1.0 + jnp.exp(-logit))
        hidden = (value / (1.0 + jnp.exp(-value)) * gate).astype(jnp.bfloat16)
        for c in range(0, CUT, JOIN):
            block = jnp.dot(
                hidden, down_ref[:, c * piece : (c + JOIN) * piece],
                preferred_element_type=jnp.float32,
            )
            for i in range(JOIN):
                for t in range(piece // lanes):
                    at = i * piece + t * lanes
                    stage[t, pl.ds(c + i, width, stride=CUT)] = block[:, at : at + lanes]
        for t in range(piece // lanes):
            partial[:, :, t * lanes : (t + 1) * lanes] = (
                stage[t].reshape(width, CUT, lanes).astype(jnp.bfloat16)
            )

    def give(owner, far, batch):
        pltpu.make_async_remote_copy(
            src_ref=partial.at[owner], dst_ref=returned.at[batch, me],
            send_sem=part_send.at[far], recv_sem=part_recv.at[batch],
            device_id=(far_pipe(far), owner), device_id_type=MESH,
        ).start()

    def pass_parts():
        each_step(lambda step: give(around(step), 1, 0))
        give(me, 1, 0)

    def share_parts():
        for far in reversed(range(1, sections)):
            give(me, far, 1)
            each_step(lambda step: give(around(step), far, 1))
        each_step(lambda step: give(around(step), 0, 1))
        pltpu.make_async_copy(partial.at[me], returned.at[1, me], part_recv.at[1]).start()

    def give_state(far, batch):
        return pltpu.make_async_remote_copy(
            src_ref=state_out, dst_ref=state_in.at[batch], send_sem=state_send.at[far],
            recv_sem=state_recv.at[batch], device_id=(far_pipe(far), me), device_id_type=MESH,
        )

    def take_state(batch):
        pltpu.make_async_copy(state_in.at[batch], state_in.at[batch], state_recv.at[batch]).wait()
        rows[...] = state_in[batch].astype(jnp.float32)

    def take_parts(phase, batch):
        pltpu.make_async_copy(returned.at[batch], returned.at[batch], part_recv.at[batch]).wait()
        updates = [
            jnp.sum(returned[batch, pl.ds(e * group, group)].astype(jnp.float32), axis=0)
            for e in range(experts)
        ]

        def apply(slot, carry):
            total = jnp.zeros((CUT, piece), jnp.float32)
            for e in range(experts):
                same = place[slot] == place[phase * experts + e]
                total += jnp.where(same, updates[e], 0.0)
            rows[slot] = (rows[slot] + total).astype(jnp.bfloat16).astype(jnp.float32)
            return carry

        lax.fori_loop(0, slots, apply, 0, unroll=slots <= 8)

    last = sections - 1

    @pl.when(section < last)
    def _():
        @pl.when(section > 0)
        def _():
            @pl.when(section > 1)
            def _():
                take_state(0)

            take_parts(section - 1, 0)
            send_rows()
            state_out[...] = rows[...].astype(jnp.bfloat16)
            give_state(1, 0).start()

        pltpu.make_async_copy(arrived, arrived, row_recv).wait()
        expert_block()
        pass_parts()

    @pl.when(section == last)
    def _():
        if last > 0:
            if last > 1:
                take_state(0)
            take_parts(section - 1, 0)
            send_rows()
            state_out[...] = rows[...].astype(jnp.bfloat16)
            for far in range(1, sections):
                give_state(far, 1).start()
        pltpu.make_async_copy(arrived, arrived, row_recv).wait()
        expert_block()
        share_parts()

    if last > 0:
        @pl.when(section < last)
        def _():
            take_state(1)

    take_parts(last, 1)

    height = slots * CUT
    wide = rows[...].reshape(height, piece)
    mean = over_cuts(jnp.sum(wide * wide, axis=1, keepdims=True)) * (1.0 / features)
    narrow = wide.astype(jnp.bfloat16)
    feats = probe_ref.shape[0]
    cut_out = lax.rem(lax.broadcasted_iota(jnp.int32, (height, feats), 0), CUT)
    changed = jnp.zeros((height, feats), jnp.float32)
    for c in range(CUT):
        term = lax.dot_general(
            narrow, probe_ref[:, c * piece : (c + 1) * piece], NT,
            preferred_element_type=jnp.float32,
        )
        changed = jnp.where(cut_out == c, term, changed)
    changed = over_cuts(changed) * lax.rsqrt(mean + EPS)
    token_id = lax.broadcasted_iota(jnp.int32, (tokens, feats), 0).astype(jnp.float32)
    result = base
    for slot in range(slots):
        at = place[slot][:1, :feats]
        result = jnp.where(token_id == at, changed[slot * CUT : slot * CUT + 1], result)
    out_ref[...] = result.astype(out_ref.dtype)

    most = returned.at[0, pl.ds(0, width - 1)]
    pltpu.make_async_copy(most, most, row_send).wait()

    @pl.when(section < last)
    def _():
        pltpu.make_async_copy(returned.at[0], returned.at[0], part_send.at[1 % sections]).wait()

        @pl.when(section > 0)
        def _():
            give_state(1, 0).wait_send()

    @pl.when(section == last)
    def _():
        pltpu.make_async_copy(most, most, part_send.at[0]).wait()
        for far in range(1, sections):
            pltpu.make_async_copy(returned.at[0], returned.at[0], part_send.at[far]).wait()
            give_state(far, 1).wait_send()


def shards(inputs, router, w_up, w_down, picks, probe):
    sections = lax.axis_size("pipe")
    width = lax.axis_size("expert")
    tokens, features = inputs.shape[1:]
    experts = router.shape[2]
    cap = picks.shape[3]
    hidden_units = w_up.shape[1]
    feats = probe.shape[1]
    piece = features // CUT
    slots = sections * experts
    any_spec = pl.BlockSpec(memory_space=pl.ANY)
    out = pl.pallas_call(
        functools.partial(kernel, sections, width, experts),
        out_shape=jax.ShapeDtypeStruct((tokens, feats), jnp.bfloat16),
        in_specs=[any_spec] * 6,
        out_specs=pl.BlockSpec(memory_space=pltpu.VMEM),
        scratch_shapes=[
            pltpu.VMEM((tokens, features), jnp.bfloat16),
            pltpu.VMEM((hidden_units + PAD, features), jnp.bfloat16),
            pltpu.VMEM((hidden_units, features), jnp.bfloat16),
            pltpu.VMEM((feats, features), jnp.bfloat16),
            pltpu.VMEM((experts, features), jnp.bfloat16),
            pltpu.VMEM((sections, experts, cap), jnp.int32),
            pltpu.VMEM((slots, CUT, piece), jnp.float32),
            pltpu.VMEM((slots, CUT, piece), jnp.float32),
            pltpu.VMEM((experts, CUT, piece), jnp.bfloat16),
            pltpu.VMEM((width, CUT, piece), jnp.bfloat16),
            pltpu.VMEM((piece // 128, width * CUT, 128), jnp.float32),
            pltpu.VMEM((width, CUT, piece), jnp.bfloat16),
            pltpu.VMEM((2, width, CUT, piece), jnp.bfloat16),
            pltpu.VMEM((slots, CUT, piece), jnp.bfloat16),
            pltpu.VMEM((2, slots, CUT, piece), jnp.bfloat16),
            pltpu.SemaphoreType.DMA((6,)),
            pltpu.SemaphoreType.DMA((sections,)),
            pltpu.SemaphoreType.DMA((sections,)),
            pltpu.SemaphoreType.DMA,
            pltpu.SemaphoreType.DMA,
            pltpu.SemaphoreType.DMA((sections,)),
            pltpu.SemaphoreType.DMA((2,)),
            pltpu.SemaphoreType.DMA((sections,)),
            pltpu.SemaphoreType.DMA((2,)),
        ],
        compiler_params=pltpu.CompilerParams(collective_id=0, has_side_effects=True),
        name="relay",
    )(inputs[0], jnp.transpose(router[0]), w_up[0], w_down[0], picks[0, 0], probe[0])
    return out[None, None]


def solution(mesh):
    return jax.shard_map(
        shards,
        mesh=mesh,
        in_specs=(
            P(None, "expert", None),
            P("pipe", None, None),
            P("pipe", "expert", None),
            P("pipe", "expert", None),
            P("pipe", None, None, None),
            P("pipe", None, None),
        ),
        out_specs=P("pipe", None, "expert", None),
        check_vma=False,
    )
```
